32 devices in a mesh: groups: 2 (over x), depth: 2 (over core), row: 8 (over z, y).
Axes of the slice: x: 2, y: 2, z: 4, core: 2. Of those that a mesh axis runs over, the one named last changes fastest.
Arguments:
- planes: float32 [4, 4, 512, 512], P('groups', None, 'row'), parts along dimension 0, may hold values from -6 to 6
- slowness: float32 [2, 512, 512], P('depth', 'row'), may hold values from 0.6 to 1.4
- ref_slowness: float32 [2], replicated, may hold values from 0.8 to 1.2
- freq_index: int32 [2], replicated, may hold values from 10 to 51
Outputs:
- image: float32 [4, 512, 512], P(('groups', 'depth'), 'row'), parts along dimension 0
- leaving: float32 [4, 4, 512, 512], P(('groups', 'depth'), None, 'row'), parts along dimension 0
The draws below stay inside these ranges and needn't reach their ends.
There are 2 independent parts, one for each index of `groups`. The reference program is written for one: setup_inputs(seed, part) draws one part's arguments, and reference() takes and returns one part's arrays. A program takes and returns all parts, laid end to end along the dimension named above; an argument that names none is the same for every part. Nothing has to cross between parts.
All inputs are finite; a program needn't handle non-finite values.
Results may differ from the reference program's by a relative error of at most 0.0003.
Values sent between devices are 32-bit elements; how exact they have to be, the bound alone decides.
A program may use at most 64 MiB of HBM per device.

```python
import jax
import jax.numpy as jnp
from jax import lax

GRID = 512
FREQS = 2
NZ = 2


def steps_of(own_key, dims, cuts, smallest, largest):
    factor_of = 1.0
    for axis_at, shards_of in cuts:
        heights = jax.random.uniform(jax.random.fold_in(jax.random.fold_in(own_key, 6), axis_at), (shards_of,), jnp.float32, smallest / len(cuts), largest / len(cuts))
        factor_of = factor_of * jnp.repeat(jnp.exp(heights), dims[axis_at] // shards_of).reshape((-1,) + (1,) * (len(dims) - 1 - axis_at))
    return factor_of


def noise(rng, dims, width, most, cuts=(), kind=jnp.bfloat16):
    values = jax.random.normal(rng, dims, jnp.float32) * width
    if len(cuts) > 0:
        values = steps_of(rng, dims, cuts, -0.22, 0.18) * values
    return jnp.clip(values, min=-most, max=most).astype(kind)


def setup_inputs(seed: int = 0, part: int = 0) -> dict:
    key_list = jax.random.split(jax.random.key(seed), 5)
    part_keys = jax.random.split(jax.random.fold_in(key_list[4], part), 5)
    planes = noise(part_keys[0], (FREQS, 4, GRID, GRID), 1.0, 6.0, ((2, 8),), jnp.float32)
    slowness = jnp.clip(0.6 + 0.79999995 * jax.random.uniform(key_list[1], (NZ, GRID, GRID), jnp.float32) ** steps_of(key_list[1], (NZ, GRID, GRID), ((0, 2), (1, 8)), -0.2, 0.2), 0.6, 1.4)
    ref_slowness = jnp.clip(jax.random.uniform(key_list[2], (NZ,), jnp.float32, 0.8, 1.2), 0.8, 1.2)
    freq_index = jax.random.randint(key_list[3], (FREQS,), 10, 52).astype(jnp.int32)
    return {"planes": planes, "slowness": slowness, "ref_slowness": ref_slowness, "freq_index": freq_index}


omega_step = 0.05
depth_step = 1.0

def wavenumbers():
    positions = jnp.arange(GRID, dtype=jnp.int32)
    signed = jnp.where(positions < GRID // 2, positions, positions - GRID)
    return 2.0 * jnp.pi / GRID * signed.astype(jnp.float32)

def reference(planes, slowness, ref_slowness, freq_index):
    waves = wavenumbers()
    plane_waves = waves[:, None] ** 2 + waves[None, :] ** 2
    omegas = omega_step * freq_index.astype(jnp.float32)
    source = planes[:, 0] + 1j * planes[:, 1]
    receiver = planes[:, 2] + 1j * planes[:, 3]
    images = []
    for level in range(NZ):
        radicand = (omegas[:, None, None] * ref_slowness[level]) ** 2 - plane_waves[None]
        vertical = jnp.sqrt(jnp.maximum(radicand, 0.0)) * depth_step
        damping = jnp.exp(-jnp.sqrt(jnp.maximum(-radicand, 0.0)) * depth_step)
        source = jnp.fft.ifft2(jnp.fft.fft2(source) * (damping * jnp.cos(vertical) - 1j * damping * jnp.sin(vertical)))
        receiver = jnp.fft.ifft2(jnp.fft.fft2(receiver) * (damping * jnp.cos(vertical) + 1j * damping * jnp.sin(vertical)))
        screen_phase = omegas[:, None, None] * (slowness[level] - ref_slowness[level])[None] * depth_step
        source = source * (jnp.cos(screen_phase) - 1j * jnp.sin(screen_phase))
        receiver = receiver * (jnp.cos(screen_phase) + 1j * jnp.sin(screen_phase))
        images.append(lax.optimization_barrier(jnp.sum(source.real * receiver.real + source.imag * receiver.imag, axis=0)))
    leaving = jnp.stack([source.real, source.imag, receiver.real, receiver.imag], axis=1)
    return (jnp.stack(images), leaving)
```

```python
import functools

import jax
import jax.numpy as jnp
import numpy as np
from jax import lax
from jax.experimental import pallas as pl
from jax.experimental.pallas import tpu as pltpu
from jax.sharding import PartitionSpec as P

OMEGA_STEP = 0.05
DEPTH_STEP = 1.0
MESH = pl.DeviceIdType.MESH
BF16 = jnp.bfloat16
F32 = jnp.float32


def dft_tables(length):
    index = np.arange(length)
    angles = 2.0 * np.pi / length * (index[:, None] * index[None, :] % length)
    parts = []
    for table in (np.cos(angles), np.sin(angles)):
        head = table.astype(BF16)
        parts += [head, (table - head.astype(np.float64)).astype(BF16)]
    return np.stack(parts)


def split(value):
    head = value.astype(BF16)
    return head, (value - head.astype(F32)).astype(BF16)


def dot(a, b):
    return jnp.dot(a, b, preferred_element_type=F32)


def kernel(
    n,
    depth,
    planes_hbm,
    slow_hbm,
    ref_slow,
    freq,
    tables_hbm,
    image_out,
    leaving_out,
    tables,
    fields,
    screens,
    prop,
    phase,
    fsend,
    frecv,
    bsend,
    brecv,
    terms,
    partner_terms,
    load_sem,
    send_sem,
    recv_sem,
    own_sem,
    slow_send,
    slow_recv,
    term_send,
    term_recv,
):
    me = lax.axis_index("row")
    seg = lax.axis_index("depth")
    grid = tables.shape[1]
    rows = grid // n
    cols = rows
    width = fsend.shape[-1]
    kp = width // 2
    freqs = fields.shape[0]
    levels = screens.shape[0]
    own_levels = levels // depth
    order = sorted(range(1, n), key=lambda d: (abs(2 * d - n), d))

    loads = []
    for at, (src, dst) in enumerate(
        [(tables_hbm, tables), (planes_hbm.at[pl.ds(seg * freqs, freqs)], fields)]
    ):
        copy = pltpu.make_async_copy(src, dst, load_sem.at[at])
        copy.start()
        loads.append(copy)
    own_slots = pl.ds(seg * own_levels, own_levels)
    slow_copy = pltpu.make_async_copy(slow_hbm, screens.at[own_slots], load_sem.at[2])
    slow_copy.start()

    barrier = pltpu.get_barrier_semaphore()
    for d in range(1, n):
        pl.semaphore_signal(
            barrier, inc=1, device_id={"row": lax.rem(me + d, n)}, device_id_type=MESH
        )
    for d in range(1, depth):
        pl.semaphore_signal(
            barrier, inc=1, device_id={"depth": lax.rem(seg + d, depth)}, device_id_type=MESH
        )

    def right(value, sign):
        head, tail = split(value)
        count = head.shape[0]
        both = jnp.concatenate([head, tail], axis=0)
        by_cos = dot(both, tables[0])
        by_sin = dot(both, tables[2])
        by_cos = by_cos[:count] + by_cos[count:] + dot(head, tables[1])
        by_sin = by_sin[:count] + by_sin[count:] + dot(head, tables[3])
        half = count // 2
        if sign > 0:
            return by_cos[:half] - by_sin[half:], by_cos[half:] + by_sin[:half]
        return by_cos[:half] + by_sin[half:], by_cos[half:] - by_sin[:half]

    lane = lax.broadcasted_iota(jnp.int32, (1, width), 1)
    lane_sign = jnp.where(lane < kp, 1.0, -1.0).astype(F32)

    def swap(value):
        return pltpu.roll(value, kp, 1) * lane_sign

    def left(value, sign):
        head, tail = split(value)
        turned = swap(value) if sign < 0 else -swap(value)
        turned_head, turned_tail = split(turned)
        by_head = dot(tables[0], jnp.concatenate([head, tail], axis=1)) + dot(
            tables[2], jnp.concatenate([turned_head, turned_tail], axis=1)
        )
        by_tail = dot(tables[1], head) + dot(tables[3], turned_head)
        return by_head[:, :width] + by_head[:, width:] + by_tail

    def exchange(slot, source, target):
        own = pltpu.make_async_copy(source.at[me], target.at[me], own_sem.at[slot])
        own.start()
        copies = [own]
        for d in order:
            to = lax.rem(me + d, n)
            copy = pltpu.make_async_remote_copy(
                src_ref=source.at[to],
                dst_ref=target.at[me],
                send_sem=send_sem.at[slot, d],
                recv_sem=recv_sem.at[slot, d],
                device_id={"row": to},
                device_id_type=MESH,
            )
            copy.start()
            copies.append(copy)
        return copies

    def slot_of(level, stage, f, c):
        return ((level * 2 + stage) * freqs + f) * 2 + c

    def forward(level, f, c):
        both = fields[f, pl.ds(2 * c, 2)].reshape(2 * rows, grid)
        re, im = right(both, -1)
        at = slot_of(level, 0, f, c)
        where = (level * freqs + f) * 2 + c
        for j in range(n):
            block = slice(j * cols, (j + 1) * cols)
            parts = [re[:, block], im[:, block]]
            if cols < kp:
                pad = jnp.zeros((rows, kp - cols), F32)
                parts = [parts[0], pad, parts[1], pad]
            fsend[where, j] = jnp.concatenate(parts, axis=1)
        return exchange(at, fsend.at[where], frecv.at[where])

    def middle(level, f, c):
        where = (level * freqs + f) * 2 + c
        value = left(frecv[where].reshape(grid, width), -1)
        even, odd = prop[level * freqs + f, 0], prop[level * freqs + f, 1]
        turned = swap(value) * odd
        value = value * even + (turned if c == 0 else -turned)
        bsend[where] = left(value, 1).reshape(n, rows, width)
        return exchange(slot_of(level, 1, f, c), bsend.at[where], brecv.at[where])

    def backward(level, f, c):
        where = (level * freqs + f) * 2 + c
        blocks = [brecv[where, i] for i in range(n)]
        re = jnp.concatenate([b[:, :cols] for b in blocks], axis=1)
        im = jnp.concatenate([b[:, kp : kp + cols] for b in blocks], axis=1)
        re, im = right(jnp.concatenate([re, im], axis=0), 1)
        even, odd = phase[level * freqs + f, 0], phase[level * freqs + f, 1]
        if c == 1:
            odd = -odd
        fields[f, 2 * c] = re * even + im * odd
        fields[f, 2 * c + 1] = im * even - re * odd

    def omega_of(f):
        return OMEGA_STEP * freq[seg * freqs + f].astype(F32)

    def signed_wave(positions):
        signed = jnp.where(positions < grid // 2, positions, positions - grid)
        return 2.0 * jnp.pi / grid * signed.astype(F32)

    def propagators(level, f):
        wave_x = signed_wave(lax.broadcasted_iota(jnp.int32, (grid, width), 0))
        at = lax.broadcasted_iota(jnp.int32, (grid, width), 1)
        at = jnp.where(at < kp, at, at - kp)
        wave_y = signed_wave(me * cols + at)
        radicand = (omega_of(f) * ref_slow[level]) ** 2 - (wave_x * wave_x + wave_y * wave_y)
        vertical = jnp.sqrt(jnp.maximum(radicand, 0.0)) * DEPTH_STEP
        damping = jnp.exp(-jnp.sqrt(jnp.maximum(-radicand, 0.0)) * DEPTH_STEP)
        damping = damping * (1.0 / (grid * grid))
        prop[level * freqs + f, 0] = damping * jnp.cos(vertical)
        prop[level * freqs + f, 1] = damping * jnp.sin(vertical)

    def phases(level, f):
        theta = omega_of(f) * (screens[level] - ref_slow[level]) * DEPTH_STEP
        phase[level * freqs + f, 0] = jnp.cos(theta)
        phase[level * freqs + f, 1] = jnp.sin(theta)

    pairs = [(f, c) for f in range(freqs) for c in range(2)]
    pl.semaphore_wait(barrier, n - 1 + depth - 1)
    for copy in loads:
        copy.wait()
    pending = []
    flights = {}
    for f, c in pairs:
        flights[f, c] = forward(0, f, c)
    slow_flights = []
    for d in range(1, depth):
        copy = pltpu.make_async_remote_copy(
            src_ref=slow_hbm,
            dst_ref=screens.at[own_slots],
            send_sem=slow_send.at[d],
            recv_sem=slow_recv.at[d],
            device_id={"depth": lax.rem(seg + d, depth)},
            device_id_type=MESH,
        )
        copy.start()
        slow_flights.append(copy)
    for f in range(freqs):
        propagators(0, f)

    def arrive(copies):
        copies[0].wait()
        for copy in copies[1:]:
            copy.wait_recv()
        pending.extend(copies[1:])

    for level in range(levels):
        returns = {}
        for f, c in pairs:
            arrive(flights[f, c])
            returns[f, c] = middle(level, f, c)
        if level == 0:
            slow_copy.wait()
            for copy in slow_flights:
                copy.wait()
            for f in range(freqs):
                for at in range(levels):
                    phases(at, f)
                    if at > 0:
                        propagators(at, f)
        flights = {}
        for f, c in pairs:
            arrive(returns[f, c])
            backward(level, f, c)
            if level < levels - 1:
                flights[f, c] = forward(level + 1, f, c)
        term = None
        for f in range(freqs):
            part = fields[f, 0] * fields[f, 2] + fields[f, 1] * fields[f, 3]
            term = part if term is None else term + part
        terms[level] = term

    swaps = []
    for d in range(1, depth):
        to = lax.rem(seg + d, depth)
        copy = pltpu.make_async_remote_copy(
            src_ref=terms.at[pl.ds(to * own_levels, own_levels)],
            dst_ref=partner_terms.at[d],
            send_sem=term_send.at[d],
            recv_sem=term_recv.at[d],
            device_id={"depth": to},
            device_id_type=MESH,
        )
        copy.start()
        swaps.append(copy)
    leaving_out[...] = fields[...]
    for copy in pending:
        copy.wait_send()
    for copy in swaps:
        copy.wait()
    total = terms[own_slots]
    for d in range(1, depth):
        total = total + partner_terms[d]
    image_out[...] = total


def shards(n, depth, planes, slowness, ref_slowness, freq_index):
    grid = planes.shape[3]
    rows = grid // n
    freqs = planes.shape[0] // depth
    own_levels = slowness.shape[0]
    levels = own_levels * depth
    kp = max(rows, 64)
    width = 2 * kp
    fields = freqs * 2 * levels
    tables = jnp.asarray(dft_tables(grid))
    any_spec = pl.BlockSpec(memory_space=pl.ANY)
    smem_spec = pl.BlockSpec(memory_space=pltpu.SMEM)
    vmem_spec = pl.BlockSpec(memory_space=pltpu.VMEM)
    blocks = pltpu.VMEM((fields, n, rows, width), F32)
    return pl.pallas_call(
        functools.partial(kernel, n, depth),
        out_shape=(
            jax.ShapeDtypeStruct((own_levels, rows, grid), F32),
            jax.ShapeDtypeStruct((freqs,) + planes.shape[1:], F32),
        ),
        in_specs=[any_spec, any_spec, smem_spec, smem_spec, any_spec],
        out_specs=(vmem_spec, vmem_spec),
        scratch_shapes=[
            pltpu.VMEM(tables.shape, BF16),
            pltpu.VMEM((freqs,) + planes.shape[1:], F32),
            pltpu.VMEM((levels, rows, grid), F32),
            pltpu.VMEM((levels * freqs, 2, grid, width), F32),
            pltpu.VMEM((levels * freqs, 2, rows, grid), F32),
            blocks,
            blocks,
            blocks,
            blocks,
            pltpu.VMEM((levels, rows, grid), F32),
            pltpu.VMEM((depth, own_levels, rows, grid), F32),
            pltpu.SemaphoreType.DMA((3,)),
            pltpu.SemaphoreType.DMA((2 * fields, n)),
            pltpu.SemaphoreType.DMA((2 * fields, n)),
            pltpu.SemaphoreType.DMA((2 * fields,)),
            pltpu.SemaphoreType.DMA((depth,)),
            pltpu.SemaphoreType.DMA((depth,)),
            pltpu.SemaphoreType.DMA((depth,)),
            pltpu.SemaphoreType.DMA((depth,)),
        ],
        compiler_params=pltpu.CompilerParams(
            collective_id=0, has_side_effects=True, vmem_limit_bytes=48 * 1024 * 1024
        ),
    )(planes, slowness, ref_slowness, freq_index, tables)


def solution(mesh):
    in_specs = (P("groups", None, "row", None), P("depth", "row", None), P(), P())
    out_specs = (P(("groups", "depth"), "row", None), P(("groups", "depth"), None, "row", None))
    body = functools.partial(shards, mesh.shape["row"], mesh.shape["depth"])
    return jax.shard_map(body, mesh=mesh, in_specs=in_specs, out_specs=out_specs, check_vma=False)
```

```python
import functools

import jax
import jax.numpy as jnp
import numpy as np
from jax import lax
from jax.experimental import pallas as pl
from jax.experimental.pallas import tpu as pltpu
from jax.sharding import PartitionSpec as P

OMEGA_STEP = 0.05
DEPTH_STEP = 1.0
MESH = pl.DeviceIdType.MESH
BF16 = jnp.bfloat16
F32 = jnp.float32


def dft_tables(length):
    index = np.arange(length)
    angles = 2.0 * np.pi / length * (index[:, None] * index[None, :] % length)
    parts = []
    for table in (np.cos(angles), np.sin(angles)):
        head = table.astype(BF16)
        parts += [head, (table - head.astype(np.float64)).astype(BF16)]
    return np.stack(parts)


def split(value):
    head = value.astype(BF16)
    return head, (value - head.astype(F32)).astype(BF16)


def dot(a, b):
    return jnp.dot(a, b, preferred_element_type=F32)


def kernel(
    n,
    depth,
    planes_hbm,
    slow_hbm,
    ref_hbm,
    freq_hbm,
    tables_hbm,
    image_out,
    leaving_out,
    ref_slow,
    freq,
    tables,
    fields,
    screens,
    prop,
    phase,
    fsend,
    frecv,
    bsend,
    brecv,
    terms,
    gathered,
    load_sem,
    send_sem,
    recv_sem,
    lone_sem,
    slow_send,
    slow_recv,
    term_send,
    term_recv,
):
    row = lax.axis_index("row")
    seg = lax.axis_index("depth")
    per_band = n // depth
    band = row // per_band
    place = row % per_band * depth + seg
    home = band == seg
    grid = tables.shape[1]
    rows = grid // n
    cols = rows
    width = fsend.shape[-1]
    kp = width // 2
    freqs = fields.shape[0]
    levels = screens.shape[0]
    own_levels = levels // depth
    order = sorted(range(1, n), key=lambda d: (abs(2 * d - n), d))

    loads = []
    wanted = [
        (planes_hbm.at[pl.ds(seg * freqs, freqs)], fields),
        (tables_hbm, tables),
        (ref_hbm, ref_slow),
        (freq_hbm, freq),
    ]
    for at, (src, dst) in enumerate(wanted):
        copy = pltpu.make_async_copy(src, dst, load_sem.at[at])
        copy.start()
        loads.append(copy)

    barrier = pltpu.get_barrier_semaphore()
    for d in range(1, n * depth):
        other = (row * depth + seg + d) % (n * depth)
        pl.semaphore_signal(
            barrier, inc=1, device_id=(lax.axis_index("groups"), other % depth, other // depth),
            device_id_type=MESH,
        )

    pending = []

    def of_row(to_row, to_seg):
        return (lax.axis_index("groups"), to_seg, to_row)

    def member(which, at):
        return of_row(which * per_band + at // depth, at % depth)

    def send(src, dst, send_at, recv_at, device, when, here):
        remote = pltpu.make_async_remote_copy(
            src_ref=src, dst_ref=dst, send_sem=send_at, recv_sem=recv_at,
            device_id=device, device_id_type=MESH,
        )
        local = pltpu.make_async_copy(src, dst, recv_at)
        away = jnp.logical_and(when, jnp.logical_not(here))

        @pl.when(away)
        def _():
            remote.start()

        @pl.when(jnp.logical_and(when, here))
        def _():
            local.start()

        pending.append((remote, away))

    def right(value, sign):
        head, tail = split(value)
        count = head.shape[0]
        both = jnp.concatenate([head, tail], axis=0)
        by_cos = dot(both, tables[0])
        by_sin = dot(both, tables[2])
        by_cos = by_cos[:count] + by_cos[count:] + dot(head, tables[1])
        by_sin = by_sin[:count] + by_sin[count:] + dot(head, tables[3])
        half = count // 2
        if sign > 0:
            return by_cos[:half] - by_sin[half:], by_cos[half:] + by_sin[:half]
        return by_cos[:half] + by_sin[half:], by_cos[half:] - by_sin[:half]

    lane = lax.broadcasted_iota(jnp.int32, (1, width), 1)
    lane_sign = jnp.where(lane < kp, 1.0, -1.0).astype(F32)

    def swap(value):
        return pltpu.roll(value, kp, 1) * lane_sign

    def left(value, sign):
        head, tail = split(value)
        turned = swap(value) if sign < 0 else -swap(value)
        turned_head, turned_tail = split(turned)
        by_head = dot(tables[0], jnp.concatenate([head, tail], axis=1)) + dot(
            tables[2], jnp.concatenate([turned_head, turned_tail], axis=1)
        )
        by_tail = dot(tables[1], head) + dot(tables[3], turned_head)
        return by_head[:, :width] + by_head[:, width:] + by_tail

    def exchange(slot, source, target, device_of, own, here):
        into, index = target
        for d in order:
            to = (own + d) % n
            pltpu.make_async_remote_copy(
                src_ref=source.at[to], dst_ref=into.at[index],
                send_sem=send_sem.at[slot], recv_sem=recv_sem.at[slot],
                device_id=device_of(to), device_id_type=MESH,
            ).start()
        send(
            source.at[own], into.at[index], lone_sem.at[slot], recv_sem.at[slot],
            device_of(own), True, here,
        )
        return slot, source, into

    def arrive(flight):
        slot, _, into = flight
        pltpu.make_async_copy(into, into, recv_sem.at[slot]).wait()
        sent.append(flight)

    def slot_of(level, stage, f, c):
        return ((level * 2 + stage) * freqs + f) * 2 + c

    def forward(level, f, c):
        both = fields[f, pl.ds(2 * c, 2)].reshape(2 * rows, grid)
        re, im = right(both, -1)
        at = slot_of(level, 0, f, c)
        where = (level * freqs + f) * 2 + c
        for j in range(n):
            block = slice(j * cols, (j + 1) * cols)
            parts = [re[:, block], im[:, block]]
            if cols < kp:
                pad = jnp.zeros((rows, kp - cols), F32)
                parts = [parts[0], pad, parts[1], pad]
            fsend[where, j] = jnp.concatenate(parts, axis=1)
        if level == 0:
            return exchange(
                at, fsend.at[where], (frecv.at[where], row), lambda t: member(seg, t), place, home
            )
        return exchange(
            at, fsend.at[where], (frecv.at[where], place), lambda t: member(band, t), place, True
        )

    def middle(level, f, c):
        where = (level * freqs + f) * 2 + c
        value = left(frecv[where].reshape(grid, width), -1)
        even, odd = prop[level * freqs + f, 0], prop[level * freqs + f, 1]
        turned = swap(value) * odd
        value = value * even + (turned if c == 0 else -turned)
        bsend[where] = left(value, 1).reshape(n, rows, width)
        at = slot_of(level, 1, f, c)
        if level == levels - 1:
            return exchange(
                at, bsend.at[where], (brecv.at[where], place), lambda t: of_row(t, band), row, home
            )
        return exchange(
            at, bsend.at[where], (brecv.at[where], place), lambda t: member(band, t), place, True
        )

    def backward(level, f, c):
        where = (level * freqs + f) * 2 + c
        blocks = [brecv[where, i] for i in range(n)]
        re = jnp.concatenate([b[:, :cols] for b in blocks], axis=1)
        im = jnp.concatenate([b[:, kp : kp + cols] for b in blocks], axis=1)
        re, im = right(jnp.concatenate([re, im], axis=0), 1)
        even, odd = phase[level * freqs + f, 0], phase[level * freqs + f, 1]
        if c == 1:
            odd = -odd
        fields[f, 2 * c] = re * even + im * odd
        fields[f, 2 * c + 1] = im * even - re * odd

    def omega_of(segment, f):
        return OMEGA_STEP * freq[segment * freqs + f].astype(F32)

    def signed_wave(positions):
        signed = jnp.where(positions < grid // 2, positions, positions - grid)
        return 2.0 * jnp.pi / grid * signed.astype(F32)

    def propagators(level, f):
        wave_x = signed_wave(lax.broadcasted_iota(jnp.int32, (grid, width), 0))
        at = lax.broadcasted_iota(jnp.int32, (grid, width), 1)
        at = jnp.where(at < kp, at, at - kp)
        wave_y = signed_wave(place * cols + at)
        radicand = (omega_of(band, f) * ref_slow[level]) ** 2 - (wave_x * wave_x + wave_y * wave_y)
        vertical = jnp.sqrt(jnp.maximum(radicand, 0.0)) * DEPTH_STEP
        damping = jnp.exp(-jnp.sqrt(jnp.maximum(-radicand, 0.0)) * DEPTH_STEP)
        damping = damping * (1.0 / (grid * grid))
        prop[level * freqs + f, 0] = damping * jnp.cos(vertical)
        prop[level * freqs + f, 1] = damping * jnp.sin(vertical)

    def phases(level, f):
        theta = omega_of(band if level < levels - 1 else seg, f) * (screens[level] - ref_slow[level]) * DEPTH_STEP
        phase[level * freqs + f, 0] = jnp.cos(theta)
        phase[level * freqs + f, 1] = jnp.sin(theta)

    pairs = [(f, c) for f in range(freqs) for c in range(2)]
    sent = []
    pl.semaphore_wait(barrier, n * depth - 1)
    for level in range(levels):
        owner, at = level // own_levels, level % own_levels
        for k in range(depth):
            if level < levels - 1:
                here = jnp.logical_and(band == k, place == row)
                device = member(k, row)
            else:
                here = seg == k
                device = of_row(row, k)
            send(
                slow_hbm.at[at], screens.at[level], slow_send.at[level, k], slow_recv.at[level],
                device, seg == owner, here,
            )
    flights = {}
    loads[0].wait()
    for copy in loads[1:]:
        copy.wait()
    for f, c in pairs:
        flights[f, c] = forward(0, f, c)
    for f in range(freqs):
        propagators(0, f)

    for level in range(levels):
        returns = {}
        for f, c in pairs:
            arrive(flights[f, c])
            returns[f, c] = middle(level, f, c)
        pltpu.make_async_copy(screens.at[level], screens.at[level], slow_recv.at[level]).wait()
        for f in range(freqs):
            phases(level, f)
            if level < levels - 1:
                propagators(level + 1, f)
        flights = {}
        for f, c in pairs:
            arrive(returns[f, c])
            backward(level, f, c)
            if level < levels - 1:
                flights[f, c] = forward(level + 1, f, c)
        term = None
        for f in range(freqs):
            part = fields[f, 0] * fields[f, 2] + fields[f, 1] * fields[f, 3]
            term = part if term is None else term + part
        terms[level] = term
        owner, at = level // own_levels, level % own_levels
        if level < levels - 1:
            device = of_row(place, owner)
            here = jnp.logical_and(place == row, seg == owner)
            slot = band
        else:
            device = of_row(row, owner)
            here = seg == owner
            slot = seg
        send(
            terms.at[level], gathered.at[at, slot], term_send.at[level], term_recv.at[at],
            device, True, here,
        )

    leaving_out[...] = fields[...]
    for slot, source, _ in sent:
        remote = source.at[pl.ds(0, n - 1)]
        pltpu.make_async_copy(remote, remote, send_sem.at[slot]).wait()
    for at in range(own_levels):
        pltpu.make_async_copy(gathered.at[at], gathered.at[at], term_recv.at[at]).wait()
        total = gathered[at, 0]
        for k in range(1, depth):
            total = total + gathered[at, k]
        image_out[at] = total
    for remote, away in pending:

        @pl.when(away)
        def _(remote=remote):
            remote.wait_send()


def shards(n, depth, planes, slowness, ref_slowness, freq_index):
    grid = planes.shape[3]
    rows = grid // n
    freqs = planes.shape[0] // depth
    own_levels = slowness.shape[0]
    levels = own_levels * depth
    kp = max(rows, 64)
    width = 2 * kp
    fields = freqs * 2 * levels
    tables = jnp.asarray(dft_tables(grid))
    hbm_spec = pl.BlockSpec(memory_space=pltpu.HBM)
    vmem_spec = pl.BlockSpec(memory_space=pltpu.VMEM)
    blocks = pltpu.VMEM((fields, n, rows, width), F32)
    return pl.pallas_call(
        functools.partial(kernel, n, depth),
        out_shape=(
            jax.ShapeDtypeStruct((own_levels, rows, grid), F32),
            jax.ShapeDtypeStruct((freqs,) + planes.shape[1:], F32),
        ),
        in_specs=[hbm_spec] * 5,
        out_specs=(vmem_spec, vmem_spec),
        scratch_shapes=[
            pltpu.SMEM((levels,), F32),
            pltpu.SMEM(freq_index.shape, jnp.int32),
            pltpu.VMEM(tables.shape, BF16),
            pltpu.VMEM((freqs,) + planes.shape[1:], F32),
            pltpu.VMEM((levels, rows, grid), F32),
            pltpu.VMEM((levels * freqs, 2, grid, width), F32),
            pltpu.VMEM((levels * freqs, 2, rows, grid), F32),
            blocks,
            blocks,
            blocks,
            blocks,
            pltpu.VMEM((levels, rows, grid), F32),
            pltpu.VMEM((own_levels, depth, rows, grid), F32),
            pltpu.SemaphoreType.DMA((4,)),
            pltpu.SemaphoreType.DMA((2 * fields,)),
            pltpu.SemaphoreType.DMA((2 * fields,)),
            pltpu.SemaphoreType.DMA((2 * fields,)),
            pltpu.SemaphoreType.DMA((levels, depth)),
            pltpu.SemaphoreType.DMA((levels,)),
            pltpu.SemaphoreType.DMA((levels,)),
            pltpu.SemaphoreType.DMA((own_levels,)),
        ],
        compiler_params=pltpu.CompilerParams(
            collective_id=0, has_side_effects=True, vmem_limit_bytes=48 * 1024 * 1024
        ),
    )(planes, slowness, ref_slowness, freq_index, tables)


def solution(mesh):
    in_specs = (P("groups", None, "row", None), P("depth", "row", None), P(), P())
    out_specs = (P(("groups", "depth"), "row", None), P(("groups", "depth"), None, "row", None))
    body = functools.partial(shards, mesh.shape["row"], mesh.shape["depth"])
    return jax.shard_map(body, mesh=mesh, in_specs=in_specs, out_specs=out_specs, check_vma=False)
```

```python
import functools

import jax
import jax.numpy as jnp
import numpy as np
from jax import lax
from jax.experimental import pallas as pl
from jax.experimental.pallas import tpu as pltpu
from jax.sharding import PartitionSpec as P

OMEGA_STEP = 0.05
DEPTH_STEP = 1.0
MESH = pl.DeviceIdType.MESH
BF16 = jnp.bfloat16
F32 = jnp.float32


def dft_tables(length):
    index = np.arange(length)
    angles = 2.0 * np.pi / length * (index[:, None] * index[None, :] % length)
    parts = []
    for table in (np.cos(angles), np.sin(angles)):
        head = table.astype(BF16)
        parts += [head, (table - head.astype(np.float64)).astype(BF16)]
    return np.stack(parts)


def split(value):
    head = value.astype(BF16)
    return head, (value - head.astype(F32)).astype(BF16)


def dot(a, b):
    return jnp.dot(a, b, preferred_element_type=F32)


def kernel(
    n,
    depth,
    planes_hbm,
    slow_hbm,
    ref_hbm,
    freq_hbm,
    tables_hbm,
    image_out,
    leaving_out,
    ref_slow,
    freq,
    tables,
    fields,
    screens,
    prop,
    phase,
    fsend,
    frecv,
    bsend,
    brecv,
    terms,
    gathered,
    load_sem,
    send_sem,
    recv_sem,
    lone_sem,
    slow_send,
    slow_recv,
    term_send,
    term_recv,
    out_sem,
):
    row = lax.axis_index("row")
    seg = lax.axis_index("depth")
    per_band = n // depth
    band = row // per_band
    place = row % per_band * depth + seg
    home = band == seg
    grid = tables.shape[1]
    rows = grid // n
    cols = rows
    width = fsend.shape[-1]
    kp = width // 2
    freqs = fields.shape[0]
    levels = screens.shape[0]
    own_levels = levels // depth
    order = sorted(range(1, n), key=lambda d: (abs(2 * d - n), d))

    loads = []
    wanted = [
        (planes_hbm.at[pl.ds(seg * freqs, freqs)], fields),
        (tables_hbm, tables),
        (ref_hbm, ref_slow),
        (freq_hbm, freq),
    ]
    for at, (src, dst) in enumerate(wanted):
        copy = pltpu.make_async_copy(src, dst, load_sem.at[at])
        copy.start()
        loads.append(copy)

    barrier = pltpu.get_barrier_semaphore()
    for d in range(1, n * depth):
        other = (row * depth + seg + d) % (n * depth)
        pl.semaphore_signal(
            barrier, inc=1, device_id=(lax.axis_index("groups"), other % depth, other // depth),
            device_id_type=MESH,
        )

    pending = []

    def of_row(to_row, to_seg):
        return (lax.axis_index("groups"), to_seg, to_row)

    def member(which, at):
        return of_row(which * per_band + at // depth, at % depth)

    def send(src, dst, send_at, recv_at, device, when, here):
        remote = pltpu.make_async_remote_copy(
            src_ref=src, dst_ref=dst, send_sem=send_at, recv_sem=recv_at,
            device_id=device, device_id_type=MESH,
        )
        local = pltpu.make_async_copy(src, dst, recv_at)
        away = jnp.logical_and(when, jnp.logical_not(here))

        @pl.when(away)
        def _():
            remote.start()

        @pl.when(jnp.logical_and(when, here))
        def _():
            local.start()

        pending.append((remote, away))

    def right(value, sign):
        head, tail = split(value)
        count = head.shape[0]
        both = jnp.concatenate([head, tail], axis=0)
        by_cos = dot(both, tables[0])
        by_sin = dot(both, tables[2])
        by_cos = by_cos[:count] + by_cos[count:] + dot(head, tables[1])
        by_sin = by_sin[:count] + by_sin[count:] + dot(head, tables[3])
        half = count // 2
        if sign > 0:
            return by_cos[:half] - by_sin[half:], by_cos[half:] + by_sin[:half]
        return by_cos[:half] + by_sin[half:], by_cos[half:] - by_sin[:half]

    lane = lax.broadcasted_iota(jnp.int32, (1, width), 1)
    lane_sign = jnp.where(lane < kp, 1.0, -1.0).astype(F32)

    def swap(value):
        return pltpu.roll(value, kp, 1) * lane_sign

    def left(value, sign):
        head, tail = split(value)
        turned = swap(value) if sign < 0 else -swap(value)
        turned_head, turned_tail = split(turned)
        by_head = dot(tables[0], jnp.concatenate([head, tail], axis=1)) + dot(
            tables[2], jnp.concatenate([turned_head, turned_tail], axis=1)
        )
        by_tail = dot(tables[1], head) + dot(tables[3], turned_head)
        return by_head[:, :width] + by_head[:, width:] + by_tail

    def exchange(slot, source, target, device_of, own, here):
        into, index = target
        for d in order:
            to = (own + d) % n
            pltpu.make_async_remote_copy(
                src_ref=source.at[to], dst_ref=into.at[index],
                send_sem=send_sem.at[slot], recv_sem=recv_sem.at[slot],
                device_id=device_of(to), device_id_type=MESH,
            ).start()
        send(
            source.at[own], into.at[index], lone_sem.at[slot], recv_sem.at[slot],
            device_of(own), True, here,
        )
        return slot, source, into

    def arrive(flight):
        slot, _, into = flight
        pltpu.make_async_copy(into, into, recv_sem.at[slot]).wait()
        sent.append(flight)

    def slot_of(level, stage, f, c):
        return ((level * 2 + stage) * freqs + f) * 2 + c

    def forward(level, f, c):
        both = fields[f, pl.ds(2 * c, 2)].reshape(2 * rows, grid)
        re, im = right(both, -1)
        at = slot_of(level, 0, f, c)
        where = (level * freqs + f) * 2 + c
        for j in range(n):
            block = slice(j * cols, (j + 1) * cols)
            parts = [re[:, block], im[:, block]]
            if cols < kp:
                pad = jnp.zeros((rows, kp - cols), F32)
                parts = [parts[0], pad, parts[1], pad]
            fsend[where, j] = jnp.concatenate(parts, axis=1)
        if level == 0:
            return exchange(
                at, fsend.at[where], (frecv.at[where], row), lambda t: member(seg, t), place, home
            )
        return exchange(
            at, fsend.at[where], (frecv.at[where], place), lambda t: member(band, t), place, True
        )

    def middle(level, f, c):
        where = (level * freqs + f) * 2 + c
        value = left(frecv[where].reshape(grid, width), -1)
        even, odd = prop[level * freqs + f, 0], prop[level * freqs + f, 1]
        turned = swap(value) * odd
        value = value * even + (turned if c == 0 else -turned)
        bsend[where] = left(value, 1).reshape(n, rows, width)
        at = slot_of(level, 1, f, c)
        if level == levels - 1:
            return exchange(
                at, bsend.at[where], (brecv.at[where], place), lambda t: of_row(t, band), row, home
            )
        return exchange(
            at, bsend.at[where], (brecv.at[where], place), lambda t: member(band, t), place, True
        )

    def backward(level, f, c):
        where = (level * freqs + f) * 2 + c
        blocks = [brecv[where, i] for i in range(n)]
        re = jnp.concatenate([b[:, :cols] for b in blocks], axis=1)
        im = jnp.concatenate([b[:, kp : kp + cols] for b in blocks], axis=1)
        re, im = right(jnp.concatenate([re, im], axis=0), 1)
        even, odd = phase[level * freqs + f, 0], phase[level * freqs + f, 1]
        if c == 1:
            odd = -odd
        fields[f, 2 * c] = re * even + im * odd
        fields[f, 2 * c + 1] = im * even - re * odd

    def omega_of(segment, f):
        return OMEGA_STEP * freq[segment * freqs + f].astype(F32)

    def signed_wave(positions):
        signed = jnp.where(positions < grid // 2, positions, positions - grid)
        return 2.0 * jnp.pi / grid * signed.astype(F32)

    def propagators(level, f):
        wave_x = signed_wave(lax.broadcasted_iota(jnp.int32, (grid, width), 0))
        at = lax.broadcasted_iota(jnp.int32, (grid, width), 1)
        at = jnp.where(at < kp, at, at - kp)
        wave_y = signed_wave(place * cols + at)
        radicand = (omega_of(band, f) * ref_slow[level]) ** 2 - (wave_x * wave_x + wave_y * wave_y)
        vertical = jnp.sqrt(jnp.maximum(radicand, 0.0)) * DEPTH_STEP
        damping = jnp.exp(-jnp.sqrt(jnp.maximum(-radicand, 0.0)) * DEPTH_STEP)
        damping = damping * (1.0 / (grid * grid))
        prop[level * freqs + f, 0] = damping * jnp.cos(vertical)
        prop[level * freqs + f, 1] = damping * jnp.sin(vertical)

    def phases(level, f):
        theta = omega_of(band if level < levels - 1 else seg, f) * (screens[level] - ref_slow[level]) * DEPTH_STEP
        phase[level * freqs + f, 0] = jnp.cos(theta)
        phase[level * freqs + f, 1] = jnp.sin(theta)

    pairs = [(f, c) for f in range(freqs) for c in range(2)]
    sent = []
    pl.semaphore_wait(barrier, n * depth - 1)
    for level in range(levels):
        owner, at = level // own_levels, level % own_levels
        for k in range(depth):
            if level < levels - 1:
                here = jnp.logical_and(band == k, place == row)
                device = member(k, row)
            else:
                here = seg == k
                device = of_row(row, k)
            send(
                slow_hbm.at[at], screens.at[level], slow_send.at[level, k], slow_recv.at[level],
                device, seg == owner, here,
            )
    leaves = []
    flights = {}
    loads[0].wait()
    for copy in loads[1:]:
        copy.wait()
    for f, c in pairs:
        flights[f, c] = forward(0, f, c)
    for f in range(freqs):
        propagators(0, f)

    for level in range(levels):
        returns = {}
        for f, c in pairs:
            arrive(flights[f, c])
            returns[f, c] = middle(level, f, c)
        pltpu.make_async_copy(screens.at[level], screens.at[level], slow_recv.at[level]).wait()
        for f in range(freqs):
            phases(level, f)
            if level < levels - 1:
                propagators(level + 1, f)
        flights = {}
        for f, c in pairs:
            arrive(returns[f, c])
            backward(level, f, c)
            if level == levels - 1:
                half = pl.ds(2 * c, 2)
                copy = pltpu.make_async_copy(
                    fields.at[f, half], leaving_out.at[f, half], out_sem.at[f, c]
                )
                copy.start()
                leaves.append(copy)
            else:
                flights[f, c] = forward(level + 1, f, c)
        term = None
        for f in range(freqs):
            part = fields[f, 0] * fields[f, 2] + fields[f, 1] * fields[f, 3]
            term = part if term is None else term + part
        terms[level] = term
        owner, at = level // own_levels, level % own_levels
        if level < levels - 1:
            device = of_row(place, owner)
            here = jnp.logical_and(place == row, seg == owner)
            slot = band
        else:
            device = of_row(row, owner)
            here = seg == owner
            slot = seg
        send(
            terms.at[level], gathered.at[at, slot], term_send.at[level], term_recv.at[at],
            device, True, here,
        )

    for slot, source, _ in sent:
        remote = source.at[pl.ds(0, n - 1)]
        pltpu.make_async_copy(remote, remote, send_sem.at[slot]).wait()
    for at in range(own_levels):
        pltpu.make_async_copy(gathered.at[at], gathered.at[at], term_recv.at[at]).wait()
        total = gathered[at, 0]
        for k in range(1, depth):
            total = total + gathered[at, k]
        image_out[at] = total
    for copy in leaves:
        copy.wait()
    for remote, away in pending:

        @pl.when(away)
        def _(remote=remote):
            remote.wait_send()


def shards(n, depth, planes, slowness, ref_slowness, freq_index):
    grid = planes.shape[3]
    rows = grid // n
    freqs = planes.shape[0] // depth
    own_levels = slowness.shape[0]
    levels = own_levels * depth
    kp = max(rows, 64)
    width = 2 * kp
    fields = freqs * 2 * levels
    tables = jnp.asarray(dft_tables(grid))
    hbm_spec = pl.BlockSpec(memory_space=pltpu.HBM)
    vmem_spec = pl.BlockSpec(memory_space=pltpu.VMEM)
    blocks = pltpu.VMEM((fields, n, rows, width), F32)
    return pl.pallas_call(
        functools.partial(kernel, n, depth),
        out_shape=(
            jax.ShapeDtypeStruct((own_levels, rows, grid), F32),
            jax.ShapeDtypeStruct((freqs,) + planes.shape[1:], F32),
        ),
        in_specs=[hbm_spec] * 5,
        out_specs=(vmem_spec, hbm_spec),
        scratch_shapes=[
            pltpu.SMEM((levels,), F32),
            pltpu.SMEM(freq_index.shape, jnp.int32),
            pltpu.VMEM(tables.shape, BF16),
            pltpu.VMEM((freqs,) + planes.shape[1:], F32),
            pltpu.VMEM((levels, rows, grid), F32),
            pltpu.VMEM((levels * freqs, 2, grid, width), F32),
            pltpu.VMEM((levels * freqs, 2, rows, grid), F32),
            blocks,
            blocks,
            blocks,
            blocks,
            pltpu.VMEM((levels, rows, grid), F32),
            pltpu.VMEM((own_levels, depth, rows, grid), F32),
            pltpu.SemaphoreType.DMA((4,)),
            pltpu.SemaphoreType.DMA((2 * fields,)),
            pltpu.SemaphoreType.DMA((2 * fields,)),
            pltpu.SemaphoreType.DMA((2 * fields,)),
            pltpu.SemaphoreType.DMA((levels, depth)),
            pltpu.SemaphoreType.DMA((levels,)),
            pltpu.SemaphoreType.DMA((levels,)),
            pltpu.SemaphoreType.DMA((own_levels,)),
            pltpu.SemaphoreType.DMA((freqs, 2)),
        ],
        compiler_params=pltpu.CompilerParams(
            collective_id=0, has_side_effects=True, vmem_limit_bytes=67043328
        ),
    )(planes, slowness, ref_slowness, freq_index, tables)


def solution(mesh):
    in_specs = (P("groups", None, "row", None), P("depth", "row", None), P(), P())
    out_specs = (P(("groups", "depth"), "row", None), P(("groups", "depth"), None, "row", None))
    body = functools.partial(shards, mesh.shape["row"], mesh.shape["depth"])
    return jax.shard_map(body, mesh=mesh, in_specs=in_specs, out_specs=out_specs, check_vma=False)
```

```python
import functools

import jax
import jax.numpy as jnp
import numpy as np
from jax import lax
from jax.experimental import pallas as pl
from jax.experimental.pallas import tpu as pltpu
from jax.sharding import PartitionSpec as P

OMEGA_STEP = 0.05
DEPTH_STEP = 1.0
MESH = pl.DeviceIdType.MESH
BF16 = jnp.bfloat16
F32 = jnp.float32


def dft_tables(length):
    index = np.arange(length)
    angles = 2.0 * np.pi / length * (index[:, None] * index[None, :] % length)
    parts = []
    for table in (np.cos(angles), np.sin(angles)):
        head = table.astype(BF16)
        parts += [head, (table - head.astype(np.float64)).astype(BF16)]
    return np.stack(parts)


def split(value):
    head = value.astype(BF16)
    return head, (value - head.astype(F32)).astype(BF16)


def dot(a, b):
    return jnp.dot(a, b, preferred_element_type=F32)


def kernel(
    n,
    depth,
    planes_hbm,
    slow_hbm,
    ref_hbm,
    freq_hbm,
    tables_hbm,
    image_out,
    leaving_out,
    ref_slow,
    freq,
    tables,
    fields,
    screens,
    prop,
    phase,
    fsend,
    frecv,
    bsend,
    brecv,
    terms,
    gathered,
    load_sem,
    send_sem,
    recv_sem,
    lone_sem,
    slow_send,
    slow_recv,
    term_send,
    term_recv,
    out_sem,
):
    row = lax.axis_index("row")
    seg = lax.axis_index("depth")
    per_band = n // depth
    band = row // per_band
    place = row % per_band * depth + seg
    home = band == seg
    grid = tables.shape[1]
    rows = grid // n
    cols = rows
    width = fsend.shape[-1]
    kp = width // 2
    freqs = fields.shape[0]
    levels = screens.shape[0]
    own_levels = levels // depth
    order = sorted(range(1, n), key=lambda d: (abs(2 * d - n), d))

    loads = []
    wanted = [
        (planes_hbm.at[pl.ds(seg * freqs, freqs)], fields),
        (tables_hbm, tables),
        (ref_hbm, ref_slow),
        (freq_hbm, freq),
    ]
    for at, (src, dst) in enumerate(wanted):
        copy = pltpu.make_async_copy(src, dst, load_sem.at[at])
        copy.start()
        loads.append(copy)

    barrier = pltpu.get_barrier_semaphore()
    for d in range(1, n * depth):
        other = (row * depth + seg + d) % (n * depth)
        pl.semaphore_signal(
            barrier, inc=1, device_id=(lax.axis_index("groups"), other % depth, other // depth),
            device_id_type=MESH,
        )

    pending = []

    def of_row(to_row, to_seg):
        return (lax.axis_index("groups"), to_seg, to_row)

    def member(which, at):
        return of_row(which * per_band + at // depth, at % depth)

    def send(src, dst, send_at, recv_at, device, when, here):
        remote = pltpu.make_async_remote_copy(
            src_ref=src, dst_ref=dst, send_sem=send_at, recv_sem=recv_at,
            device_id=device, device_id_type=MESH,
        )
        local = pltpu.make_async_copy(src, dst, recv_at)
        away = jnp.logical_and(when, jnp.logical_not(here))

        @pl.when(away)
        def _():
            remote.start()

        @pl.when(jnp.logical_and(when, here))
        def _():
            local.start()

        pending.append((remote, away))

    def right(value, sign):
        head, tail = split(value)
        count = head.shape[0]
        both = jnp.concatenate([head, tail], axis=0)
        by_cos = dot(both, tables[0])
        by_sin = dot(both, tables[2])
        by_cos = by_cos[:count] + by_cos[count:] + dot(head, tables[1])
        by_sin = by_sin[:count] + by_sin[count:] + dot(head, tables[3])
        half = count // 2
        if sign > 0:
            return by_cos[:half] - by_sin[half:], by_cos[half:] + by_sin[:half]
        return by_cos[:half] + by_sin[half:], by_cos[half:] - by_sin[:half]

    lane = lax.broadcasted_iota(jnp.int32, (1, width), 1)
    lane_sign = jnp.where(lane < kp, 1.0, -1.0).astype(F32)

    def swap(value):
        return pltpu.roll(value, kp, 1) * lane_sign

    def left(value, sign):
        head, tail = split(value)
        turned = swap(value) if sign < 0 else -swap(value)
        turned_head, turned_tail = split(turned)
        by_head = dot(tables[0], jnp.concatenate([head, tail], axis=1)) + dot(
            tables[2], jnp.concatenate([turned_head, turned_tail], axis=1)
        )
        by_tail = dot(tables[1], head) + dot(tables[3], turned_head)
        return by_head[:, :width] + by_head[:, width:] + by_tail

    def exchange(slot, source, target, device_of, own, here):
        into, index = target
        for d in order:
            to = (own + d) % n
            pltpu.make_async_remote_copy(
                src_ref=source.at[to], dst_ref=into.at[index],
                send_sem=send_sem.at[slot], recv_sem=recv_sem.at[slot],
                device_id=device_of(to), device_id_type=MESH,
            ).start()
        send(
            source.at[own], into.at[index], lone_sem.at[slot], recv_sem.at[slot],
            device_of(own), True, here,
        )
        return slot, source, into

    def arrive(flight):
        slot, _, into = flight
        pltpu.make_async_copy(into, into, recv_sem.at[slot]).wait()
        sent.append(flight)

    def slot_of(level, stage, f, c):
        return ((level * 2 + stage) * freqs + f) * 2 + c

    def forward(level, f, c):
        both = fields[f, pl.ds(2 * c, 2)].reshape(2 * rows, grid)
        re, im = right(both, -1)
        at = slot_of(level, 0, f, c)
        where = (level * freqs + f) * 2 + c
        for j in range(n):
            block = slice(j * cols, (j + 1) * cols)
            parts = [re[:, block], im[:, block]]
            if cols < kp:
                pad = jnp.zeros((rows, kp - cols), F32)
                parts = [parts[0], pad, parts[1], pad]
            fsend[where, j] = jnp.concatenate(parts, axis=1)
        if level == 0:
            return exchange(
                at, fsend.at[where], (frecv.at[where], row), lambda t: member(seg, t), place, home
            )
        return exchange(
            at, fsend.at[where], (frecv.at[where], place), lambda t: member(band, t), place, True
        )

    def middle(level, f, c):
        where = (level * freqs + f) * 2 + c
        value = left(frecv[where].reshape(grid, width), -1)
        even, odd = prop[level * freqs + f, 0], prop[level * freqs + f, 1]
        turned = swap(value) * odd
        value = value * even + (turned if c == 0 else -turned)
        bsend[where] = left(value, 1).reshape(n, rows, width)
        at = slot_of(level, 1, f, c)
        if level == levels - 1:
            return exchange(
                at, bsend.at[where], (brecv.at[where], place), lambda t: of_row(t, band), row, home
            )
        return exchange(
            at, bsend.at[where], (brecv.at[where], place), lambda t: member(band, t), place, True
        )

    def backward(level, f, c):
        where = (level * freqs + f) * 2 + c
        blocks = [brecv[where, i] for i in range(n)]
        re = jnp.concatenate([b[:, :cols] for b in blocks], axis=1)
        im = jnp.concatenate([b[:, kp : kp + cols] for b in blocks], axis=1)
        re, im = right(jnp.concatenate([re, im], axis=0), 1)
        even, odd = phase[level * freqs + f, 0], phase[level * freqs + f, 1]
        if c == 1:
            odd = -odd
        fields[f, 2 * c] = re * even + im * odd
        fields[f, 2 * c + 1] = im * even - re * odd

    def omega_of(segment, f):
        return OMEGA_STEP * freq[segment * freqs + f].astype(F32)

    def signed_wave(positions):
        signed = jnp.where(positions < grid // 2, positions, positions - grid)
        return 2.0 * jnp.pi / grid * signed.astype(F32)

    def propagators(level, f):
        wave_x = signed_wave(lax.broadcasted_iota(jnp.int32, (grid, width), 0))
        at = lax.broadcasted_iota(jnp.int32, (grid, width), 1)
        at = jnp.where(at < kp, at, at - kp)
        wave_y = signed_wave(place * cols + at)
        radicand = (omega_of(band, f) * ref_slow[level]) ** 2 - (wave_x * wave_x + wave_y * wave_y)
        vertical = jnp.sqrt(jnp.maximum(radicand, 0.0)) * DEPTH_STEP
        damping = jnp.exp(-jnp.sqrt(jnp.maximum(-radicand, 0.0)) * DEPTH_STEP)
        damping = damping * (1.0 / (grid * grid))
        prop[level * freqs + f, 0] = damping * jnp.cos(vertical)
        prop[level * freqs + f, 1] = damping * jnp.sin(vertical)

    def phases(level, f):
        theta = omega_of(band if level < levels - 1 else seg, f) * (screens[level] - ref_slow[level]) * DEPTH_STEP
        phase[level * freqs + f, 0] = jnp.cos(theta)
        phase[level * freqs + f, 1] = jnp.sin(theta)

    pairs = [(f, c) for f in range(freqs) for c in range(2)]
    sent = []
    pl.semaphore_wait(barrier, n * depth - 1)
    leaves = []
    flights = {}
    for copy in loads:
        copy.wait()
    for f, c in pairs:
        flights[f, c] = forward(0, f, c)
    for level in range(levels):
        owner, at = level // own_levels, level % own_levels
        for k in range(depth):
            if level < levels - 1:
                here = jnp.logical_and(band == k, place == row)
                device = member(k, row)
            else:
                here = seg == k
                device = of_row(row, k)
            send(
                slow_hbm.at[at], screens.at[level], slow_send.at[level, k], slow_recv.at[level],
                device, seg == owner, here,
            )
    for f in range(freqs):
        propagators(0, f)

    for level in range(levels):
        returns = {}
        for f, c in pairs:
            arrive(flights[f, c])
            returns[f, c] = middle(level, f, c)
        pltpu.make_async_copy(screens.at[level], screens.at[level], slow_recv.at[level]).wait()
        for f in range(freqs):
            phases(level, f)
            if level < levels - 1:
                propagators(level + 1, f)
        flights = {}
        for f, c in pairs:
            arrive(returns[f, c])
            backward(level, f, c)
            if level == levels - 1:
                half = pl.ds(2 * c, 2)
                copy = pltpu.make_async_copy(
                    fields.at[f, half], leaving_out.at[f, half], out_sem.at[f, c]
                )
                copy.start()
                leaves.append(copy)
            else:
                flights[f, c] = forward(level + 1, f, c)
        term = None
        for f in range(freqs):
            part = fields[f, 0] * fields[f, 2] + fields[f, 1] * fields[f, 3]
            term = part if term is None else term + part
        terms[level] = term
        owner, at = level // own_levels, level % own_levels
        if level < levels - 1:
            device = of_row(place, owner)
            here = jnp.logical_and(place == row, seg == owner)
            slot = band
        else:
            device = of_row(row, owner)
            here = seg == owner
            slot = seg
        send(
            terms.at[level], gathered.at[at, slot], term_send.at[level], term_recv.at[at],
            device, True, here,
        )

    for slot, source, _ in sent:
        remote = source.at[pl.ds(0, n - 1)]
        pltpu.make_async_copy(remote, remote, send_sem.at[slot]).wait()
    for at in range(own_levels):
        pltpu.make_async_copy(gathered.at[at], gathered.at[at], term_recv.at[at]).wait()
        total = gathered[at, 0]
        for k in range(1, depth):
            total = total + gathered[at, k]
        image_out[at] = total
    for copy in leaves:
        copy.wait()
    for remote, away in pending:

        @pl.when(away)
        def _(remote=remote):
            remote.wait_send()


def shards(n, depth, planes, slowness, ref_slowness, freq_index):
    grid = planes.shape[3]
    rows = grid // n
    freqs = planes.shape[0] // depth
    own_levels = slowness.shape[0]
    levels = own_levels * depth
    kp = max(rows, 64)
    width = 2 * kp
    fields = freqs * 2 * levels
    tables = jnp.asarray(dft_tables(grid))
    hbm_spec = pl.BlockSpec(memory_space=pltpu.HBM)
    vmem_spec = pl.BlockSpec(memory_space=pltpu.VMEM)
    blocks = pltpu.VMEM((fields, n, rows, width), F32)
    return pl.pallas_call(
        functools.partial(kernel, n, depth),
        out_shape=(
            pltpu.VMEM((own_levels, rows, grid), F32),
            pltpu.VMEM((freqs,) + planes.shape[1:], F32),
        ),
        in_specs=[hbm_spec] * 5,
        out_specs=(vmem_spec, vmem_spec),
        scratch_shapes=[
            pltpu.SMEM((levels,), F32),
            pltpu.SMEM(freq_index.shape, jnp.int32),
            pltpu.VMEM(tables.shape, BF16),
            pltpu.VMEM((freqs,) + planes.shape[1:], F32),
            pltpu.VMEM((levels, rows, grid), F32),
            pltpu.VMEM((levels * freqs, 2, grid, width), F32),
            pltpu.VMEM((levels * freqs, 2, rows, grid), F32),
            blocks,
            blocks,
            blocks,
            blocks,
            pltpu.VMEM((levels, rows, grid), F32),
            pltpu.VMEM((own_levels, depth, rows, grid), F32),
            pltpu.SemaphoreType.DMA((4,)),
            pltpu.SemaphoreType.DMA((2 * fields,)),
            pltpu.SemaphoreType.DMA((2 * fields,)),
            pltpu.SemaphoreType.DMA((2 * fields,)),
            pltpu.SemaphoreType.DMA((levels, depth)),
            pltpu.SemaphoreType.DMA((levels,)),
            pltpu.SemaphoreType.DMA((levels,)),
            pltpu.SemaphoreType.DMA((own_levels,)),
            pltpu.SemaphoreType.DMA((freqs, 2)),
        ],
        compiler_params=pltpu.CompilerParams(
            collective_id=0, has_side_effects=True, vmem_limit_bytes=67043328 - (1 << 20)
        ),
    )(planes, slowness, ref_slowness, freq_index, tables)


def solution(mesh):
    in_specs = (P("groups", None, "row", None), P("depth", "row", None), P(), P())
    out_specs = (P(("groups", "depth"), "row", None), P(("groups", "depth"), None, "row", None))
    body = functools.partial(shards, mesh.shape["row"], mesh.shape["depth"])
    return jax.shard_map(body, mesh=mesh, in_specs=in_specs, out_specs=out_specs, check_vma=False)
```

```python
import functools

import jax
import jax.numpy as jnp
import numpy as np
from jax import lax
from jax.experimental import pallas as pl
from jax.experimental.pallas import tpu as pltpu
from jax.sharding import PartitionSpec as P

OMEGA_STEP = 0.05
DEPTH_STEP = 1.0
MESH = pl.DeviceIdType.MESH
BF16 = jnp.bfloat16
F32 = jnp.float32


def dft_tables(length):
    index = np.arange(length)
    angles = 2.0 * np.pi / length * (index[:, None] * index[None, :] % length)
    parts = []
    for table in (np.cos(angles), np.sin(angles)):
        head = table.astype(BF16)
        parts += [head, (table - head.astype(np.float64)).astype(BF16)]
    return np.stack(parts)


def split(value):
    head = value.astype(BF16)
    return head, (value - head.astype(F32)).astype(BF16)


def dot(a, b):
    return jnp.dot(a, b, preferred_element_type=F32)


def kernel(
    n,
    depth,
    planes_hbm,
    slow_hbm,
    ref_hbm,
    freq_hbm,
    tables_hbm,
    image_out,
    leaving_out,
    ref_slow,
    freq,
    tables,
    fields,
    screens,
    prop,
    phase,
    fsend,
    frecv,
    bsend,
    brecv,
    terms,
    gathered,
    load_sem,
    send_sem,
    recv_sem,
    lone_sem,
    slow_send,
    slow_recv,
    term_send,
    term_recv,
    out_sem,
):
    row = lax.axis_index("row")
    seg = lax.axis_index("depth")
    per_band = n // depth
    band = row // per_band
    place = row % per_band * depth + seg
    home = band == seg
    grid = tables.shape[1]
    rows = grid // n
    cols = rows
    width = fsend.shape[-1]
    kp = width // 2
    freqs = fields.shape[0]
    levels = screens.shape[0]
    own_levels = levels // depth
    order = range(1, n)

    loads = []
    wanted = [
        (planes_hbm.at[pl.ds(seg * freqs, freqs)], fields),
        (tables_hbm, tables),
        (ref_hbm, ref_slow),
        (freq_hbm, freq),
    ]
    for at, (src, dst) in enumerate(wanted):
        copy = pltpu.make_async_copy(src, dst, load_sem.at[at])
        copy.start()
        loads.append(copy)

    barrier = pltpu.get_barrier_semaphore()
    for d in range(1, n * depth):
        other = (row * depth + seg + d) % (n * depth)
        pl.semaphore_signal(
            barrier, inc=1, device_id=(lax.axis_index("groups"), other % depth, other // depth),
            device_id_type=MESH,
        )

    pending = []

    def of_row(to_row, to_seg):
        return (lax.axis_index("groups"), to_seg, to_row)

    def member(which, at):
        return of_row(which * per_band + at // depth, at % depth)

    def send(src, dst, send_at, recv_at, device, when, here):
        remote = pltpu.make_async_remote_copy(
            src_ref=src, dst_ref=dst, send_sem=send_at, recv_sem=recv_at,
            device_id=device, device_id_type=MESH,
        )
        local = pltpu.make_async_copy(src, dst, recv_at)
        away = jnp.logical_and(when, jnp.logical_not(here))

        @pl.when(away)
        def _():
            remote.start()

        @pl.when(jnp.logical_and(when, here))
        def _():
            local.start()

        pending.append((remote, away))

    def right(value, sign):
        head, tail = split(value)
        count = head.shape[0]
        both = jnp.concatenate([head, tail], axis=0)
        by_cos = dot(both, tables[0])
        by_sin = dot(both, tables[2])
        by_cos = by_cos[:count] + by_cos[count:] + dot(head, tables[1])
        by_sin = by_sin[:count] + by_sin[count:] + dot(head, tables[3])
        half = count // 2
        if sign > 0:
            return by_cos[:half] - by_sin[half:], by_cos[half:] + by_sin[:half]
        return by_cos[:half] + by_sin[half:], by_cos[half:] - by_sin[:half]

    lane = lax.broadcasted_iota(jnp.int32, (1, width), 1)
    lane_sign = jnp.where(lane < kp, 1.0, -1.0).astype(F32)

    def swap(value):
        return pltpu.roll(value, kp, 1) * lane_sign

    def left(value, sign):
        head, tail = split(value)
        turned = swap(value) if sign < 0 else -swap(value)
        turned_head, turned_tail = split(turned)
        by_head = dot(tables[0], jnp.concatenate([head, tail], axis=1)) + dot(
            tables[2], jnp.concatenate([turned_head, turned_tail], axis=1)
        )
        by_tail = dot(tables[1], head) + dot(tables[3], turned_head)
        return by_head[:, :width] + by_head[:, width:] + by_tail

    def exchange(slot, source, target, device_of, own, here):
        into, index = target
        for d in order:
            to = (own + d) % n
            pltpu.make_async_remote_copy(
                src_ref=source.at[to], dst_ref=into.at[index],
                send_sem=send_sem.at[slot], recv_sem=recv_sem.at[slot],
                device_id=device_of(to), device_id_type=MESH,
            ).start()
        send(
            source.at[own], into.at[index], lone_sem.at[slot], recv_sem.at[slot],
            device_of(own), True, here,
        )
        return slot, source, into

    def arrive(flight):
        slot, _, into = flight
        pltpu.make_async_copy(into, into, recv_sem.at[slot]).wait()
        sent.append(flight)

    def slot_of(level, stage, f, c):
        return ((level * 2 + stage) * freqs + f) * 2 + c

    def forward(level, f, c):
        both = fields[f, pl.ds(2 * c, 2)].reshape(2 * rows, grid)
        re, im = right(both, -1)
        at = slot_of(level, 0, f, c)
        where = (level * freqs + f) * 2 + c
        for j in range(n):
            block = slice(j * cols, (j + 1) * cols)
            parts = [re[:, block], im[:, block]]
            if cols < kp:
                pad = jnp.zeros((rows, kp - cols), F32)
                parts = [parts[0], pad, parts[1], pad]
            fsend[where, j] = jnp.concatenate(parts, axis=1)
        if level == 0:
            return exchange(
                at, fsend.at[where], (frecv.at[where], row), lambda t: member(seg, t), place, home
            )
        return exchange(
            at, fsend.at[where], (frecv.at[where], place), lambda t: member(band, t), place, True
        )

    def middle(level, f, c):
        where = (level * freqs + f) * 2 + c
        value = left(frecv[where].reshape(grid, width), -1)
        even, odd = prop[level * freqs + f, 0], prop[level * freqs + f, 1]
        turned = swap(value) * odd
        value = value * even + (turned if c == 0 else -turned)
        bsend[where] = left(value, 1).reshape(n, rows, width)
        at = slot_of(level, 1, f, c)
        if level == levels - 1:
            return exchange(
                at, bsend.at[where], (brecv.at[where], place), lambda t: of_row(t, band), row, home
            )
        return exchange(
            at, bsend.at[where], (brecv.at[where], place), lambda t: member(band, t), place, True
        )

    def backward(level, f, c):
        where = (level * freqs + f) * 2 + c
        blocks = [brecv[where, i] for i in range(n)]
        re = jnp.concatenate([b[:, :cols] for b in blocks], axis=1)
        im = jnp.concatenate([b[:, kp : kp + cols] for b in blocks], axis=1)
        re, im = right(jnp.concatenate([re, im], axis=0), 1)
        even, odd = phase[level * freqs + f, 0], phase[level * freqs + f, 1]
        if c == 1:
            odd = -odd
        fields[f, 2 * c] = re * even + im * odd
        fields[f, 2 * c + 1] = im * even - re * odd

    def omega_of(segment, f):
        return OMEGA_STEP * freq[segment * freqs + f].astype(F32)

    def signed_wave(positions):
        signed = jnp.where(positions < grid // 2, positions, positions - grid)
        return 2.0 * jnp.pi / grid * signed.astype(F32)

    def propagators(level, f):
        wave_x = signed_wave(lax.broadcasted_iota(jnp.int32, (grid, width), 0))
        at = lax.broadcasted_iota(jnp.int32, (grid, width), 1)
        at = jnp.where(at < kp, at, at - kp)
        wave_y = signed_wave(place * cols + at)
        radicand = (omega_of(band, f) * ref_slow[level]) ** 2 - (wave_x * wave_x + wave_y * wave_y)
        vertical = jnp.sqrt(jnp.maximum(radicand, 0.0)) * DEPTH_STEP
        damping = jnp.exp(-jnp.sqrt(jnp.maximum(-radicand, 0.0)) * DEPTH_STEP)
        damping = damping * (1.0 / (grid * grid))
        prop[level * freqs + f, 0] = damping * jnp.cos(vertical)
        prop[level * freqs + f, 1] = damping * jnp.sin(vertical)

    def phases(level, f):
        theta = omega_of(band if level < levels - 1 else seg, f) * (screens[level] - ref_slow[level]) * DEPTH_STEP
        phase[level * freqs + f, 0] = jnp.cos(theta)
        phase[level * freqs + f, 1] = jnp.sin(theta)

    pairs = [(f, c) for f in range(freqs) for c in range(2)]
    sent = []
    pl.semaphore_wait(barrier, n * depth - 1)
    leaves = []
    flights = {}
    for copy in loads:
        copy.wait()
    for f, c in pairs:
        flights[f, c] = forward(0, f, c)
    for level in range(levels):
        owner, at = level // own_levels, level % own_levels
        for k in range(depth):
            if level < levels - 1:
                here = jnp.logical_and(band == k, place == row)
                device = member(k, row)
            else:
                here = seg == k
                device = of_row(row, k)
            send(
                slow_hbm.at[at], screens.at[level], slow_send.at[level, k], slow_recv.at[level],
                device, seg == owner, here,
            )
    for level in range(levels):
        for f in range(freqs):
            propagators(level, f)

    for level in range(levels):
        returns = {}
        for f, c in pairs:
            arrive(flights[f, c])
            returns[f, c] = middle(level, f, c)
        pltpu.make_async_copy(screens.at[level], screens.at[level], slow_recv.at[level]).wait()
        for f in range(freqs):
            phases(level, f)
        flights = {}
        for f, c in pairs:
            arrive(returns[f, c])
            backward(level, f, c)
            if level == levels - 1:
                half = pl.ds(2 * c, 2)
                copy = pltpu.make_async_copy(
                    fields.at[f, half], leaving_out.at[f, half], out_sem.at[f, c]
                )
                copy.start()
                leaves.append(copy)
            else:
                flights[f, c] = forward(level + 1, f, c)
        term = None
        for f in range(freqs):
            part = fields[f, 0] * fields[f, 2] + fields[f, 1] * fields[f, 3]
            term = part if term is None else term + part
        terms[level] = term
        owner, at = level // own_levels, level % own_levels
        if level < levels - 1:
            device = of_row(place, owner)
            here = jnp.logical_and(place == row, seg == owner)
            slot = band
        else:
            device = of_row(row, owner)
            here = seg == owner
            slot = seg
        send(
            terms.at[level], gathered.at[at, slot], term_send.at[level], term_recv.at[at],
            device, True, here,
        )

    for slot, source, _ in sent:
        remote = source.at[pl.ds(0, n - 1)]
        pltpu.make_async_copy(remote, remote, send_sem.at[slot]).wait()
    for at in range(own_levels):
        pltpu.make_async_copy(gathered.at[at], gathered.at[at], term_recv.at[at]).wait()
        total = gathered[at, 0]
        for k in range(1, depth):
            total = total + gathered[at, k]
        image_out[at] = total
    for copy in leaves:
        copy.wait()
    for remote, away in pending:

        @pl.when(away)
        def _(remote=remote):
            remote.wait_send()


def shards(n, depth, planes, slowness, ref_slowness, freq_index):
    grid = planes.shape[3]
    rows = grid // n
    freqs = planes.shape[0] // depth
    own_levels = slowness.shape[0]
    levels = own_levels * depth
    kp = max(rows, 64)
    width = 2 * kp
    fields = freqs * 2 * levels
    tables = jnp.asarray(dft_tables(grid))
    hbm_spec = pl.BlockSpec(memory_space=pltpu.HBM)
    vmem_spec = pl.BlockSpec(memory_space=pltpu.VMEM)
    blocks = pltpu.VMEM((fields, n, rows, width), F32)
    return pl.pallas_call(
        functools.partial(kernel, n, depth),
        out_shape=(
            pltpu.VMEM((own_levels, rows, grid), F32),
            pltpu.VMEM((freqs,) + planes.shape[1:], F32),
        ),
        in_specs=[hbm_spec] * 5,
        out_specs=(vmem_spec, vmem_spec),
        scratch_shapes=[
            pltpu.SMEM((levels,), F32),
            pltpu.SMEM(freq_index.shape, jnp.int32),
            pltpu.VMEM(tables.shape, BF16),
            pltpu.VMEM((freqs,) + planes.shape[1:], F32),
            pltpu.VMEM((levels, rows, grid), F32),
            pltpu.VMEM((levels * freqs, 2, grid, width), F32),
            pltpu.VMEM((levels * freqs, 2, rows, grid), F32),
            blocks,
            blocks,
            blocks,
            blocks,
            pltpu.VMEM((levels, rows, grid), F32),
            pltpu.VMEM((own_levels, depth, rows, grid), F32),
            pltpu.SemaphoreType.DMA((4,)),
            pltpu.SemaphoreType.DMA((2 * fields,)),
            pltpu.SemaphoreType.DMA((2 * fields,)),
            pltpu.SemaphoreType.DMA((2 * fields,)),
            pltpu.SemaphoreType.DMA((levels, depth)),
            pltpu.SemaphoreType.DMA((levels,)),
            pltpu.SemaphoreType.DMA((levels,)),
            pltpu.SemaphoreType.DMA((own_levels,)),
            pltpu.SemaphoreType.DMA((freqs, 2)),
        ],
        compiler_params=pltpu.CompilerParams(
            collective_id=0, has_side_effects=True, vmem_limit_bytes=67043328 - (1 << 20)
        ),
    )(planes, slowness, ref_slowness, freq_index, tables)


def solution(mesh):
    in_specs = (P("groups", None, "row", None), P("depth", "row", None), P(), P())
    out_specs = (P(("groups", "depth"), "row", None), P(("groups", "depth"), None, "row", None))
    body = functools.partial(shards, mesh.shape["row"], mesh.shape["depth"])
    return jax.shard_map(body, mesh=mesh, in_specs=in_specs, out_specs=out_specs, check_vma=False)
```
